32 devices in a mesh: dp: 16 (over z, y, core), mp: 2 (over x).
Axes of the slice: x: 2, y: 2, z: 4, core: 2. Of those that a mesh axis runs over, the one named last changes fastest.
Arguments:
- tokens: bfloat16 [32768, 768], P(('dp', 'mp')), may hold values from -6 to 6
- lengths: int32 [64], P(('dp', 'mp')), may hold values from 32 to 512, as said below
- w_in: bfloat16 [768, 2304], P(('dp', 'mp')), may hold values from -0.21875 to 0.21875
- w_out: bfloat16 [768, 768], P(('dp', 'mp')), may hold values from -0.21875 to 0.21875
- short_conv: bfloat16 [3, 2304], P(None, ('dp', 'mp')), may hold values from -3 to 3
- cond_conv: bfloat16 [3, 768], P(None, ('dp', 'mp')), may hold values from -3 to 3
- cond_gain: bfloat16 [2, 513, 768], P(None, None, ('dp', 'mp')), may hold values from -0.29882812 to 0.29882812
- base_spectrum: bfloat16 [2, 513, 768], P(None, None, ('dp', 'mp')), may hold values from -4 to 4
- gain1: bfloat16 [768], P(('dp', 'mp')), may hold values from 0.5 to 1.5
- gain2: bfloat16 [768], P(('dp', 'mp')), may hold values from 0.5 to 1.5
- w_gate: bfloat16 [768, 3072], P('dp', 'mp'), may hold values from -0.21875 to 0.21875
- w_up: bfloat16 [768, 3072], P('dp', 'mp'), may hold values from -0.21875 to 0.21875
- w_down: bfloat16 [3072, 768], P('mp', 'dp'), may hold values from -0.109375 to 0.109375
- cotangent: bfloat16 [32768, 768], P(('dp', 'mp')), may hold values from -6 to 6
Outputs:
- mixed: bfloat16 [32768, 768], P(('dp', 'mp'))
- grad_tokens: float32 [32768, 768], P(('dp', 'mp'))
- grad_w_in: float32 [768, 2304], P(('dp', 'mp'))
- grad_w_out: float32 [768, 768], P(('dp', 'mp'))
- grad_short_conv: float32 [3, 2304], P(None, ('dp', 'mp'))
- grad_cond_conv: float32 [3, 768], P(None, ('dp', 'mp'))
- grad_cond_gain: float32 [2, 513, 768], P(None, None, ('dp', 'mp'))
- grad_base_spectrum: float32 [2, 513, 768], P(None, None, ('dp', 'mp'))
- grad_gain1: float32 [768], P(('dp', 'mp'))
- grad_gain2: float32 [768], P(('dp', 'mp'))
- grad_w_gate: float32 [768, 3072], P('dp', 'mp')
- grad_w_up: float32 [768, 3072], P('dp', 'mp')
- grad_w_down: float32 [3072, 768], P('mp', 'dp')
The draws below stay inside these ranges and needn't reach their ends.
Inputs may be any that keep to these rules, and one draw needn't show every extreme that they name: `lengths`: each sequence's length; slots at and beyond it are padding; some sequence has 512 and some 32.
All inputs are finite; a program needn't handle non-finite values.
Results may differ from the reference program's by a relative error of at most 0.015.
Values may be sent and summed in bfloat16 or wider, within the bound.
No kernel may reach another device: no remote copies, remote signals or barrier semaphores. Data moves between devices by JAX's collectives and lax.ppermute only.
A program may use at most 320 MiB of HBM per device.

```python
import math
import jax
import jax.numpy as jnp
from jax import lax

D = 768
FF = 3072
LENGTH = 512
MIN_LEN = 32
SEQS = 64
TOKENS = 32768
BINS = 513


def draw_lengths(key, part):
    key_r = jax.random.fold_in(key, 11)
    key_a = jax.random.fold_in(key, 12)
    key_b = jax.random.fold_in(key, 13)
    span = LENGTH - MIN_LEN
    draws = jax.random.randint(key_r, (SEQS,), 0, span + 1)
    lens = LENGTH - draws * draws // max(span, 1)
    first = jax.random.randint(key_a, (), 0, SEQS)
    second = (first + 1 + jax.random.randint(key_b, (), 0, SEQS - 1)) % SEQS
    places = jnp.arange(SEQS, dtype=jnp.int32)
    lens = jnp.where(places == first, LENGTH, lens)
    lens = jnp.where(places == second, MIN_LEN, lens)
    return lens.astype(jnp.int32)


def level_of(own_key, extent, cuts, least, top_value):
    loudness, own = 1.0, jax.random.fold_in(own_key, 6)
    for position, shards_of in cuts:
        heights = jnp.exp(jax.random.uniform(jax.random.fold_in(own, position), (shards_of,), jnp.float32, least / len(cuts), top_value / len(cuts)))
        loudness = loudness * jnp.repeat(heights, extent[position] // shards_of).reshape([-1 if axis == position else 1 for axis in range(len(extent))])
    return loudness


def bell_draw(key, shape, scale, limit, cuts=(), held_as=jnp.bfloat16):
    level = level_of(key, shape, cuts, -0.22, 0.18) if cuts else 1.0
    entries = jax.random.normal(key, shape, jnp.float32) * scale * level
    return jnp.minimum(jnp.maximum(entries, -limit), limit).astype(held_as)


def setup_inputs(seed: int = 0) -> dict:
    splits = jax.random.split(jax.random.key(seed), 15)
    tokens = bell_draw(splits[0], (TOKENS, D), 1.0, 6.0, ((0, 32),))
    lengths = draw_lengths(jax.random.fold_in(splits[14], 71), 0)
    w_in = bell_draw(splits[2], (D, 3 * D), D ** -0.5, 0.21875, ((0, 32),))
    w_out = bell_draw(splits[3], (D, D), D ** -0.5, 0.21875, ((0, 32),))
    short_conv = bell_draw(splits[4], (3, 3 * D), 0.6, 3.0, ((1, 32),))
    cond_conv = bell_draw(splits[5], (3, D), 0.6, 3.0, ((1, 32),))
    cond_gain = bell_draw(splits[6], (2, BINS, D), 0.05, 0.29882812, ((2, 32),))
    base_spectrum = bell_draw(splits[7], (2, BINS, D), 0.7, 4.0, ((2, 32),))
    gain1 = jnp.clip(1.0 + 0.1 * jax.random.normal(splits[8], (D,), jnp.float32), 0.5, 1.5).astype(jnp.bfloat16)
    gain2 = jnp.clip(1.0 + 0.1 * jax.random.normal(splits[9], (D,), jnp.float32), 0.5, 1.5).astype(jnp.bfloat16)
    w_gate = bell_draw(splits[10], (D, FF), D ** -0.5, 0.21875, ((0, 16), (1, 2)))
    w_up = bell_draw(splits[11], (D, FF), D ** -0.5, 0.21875, ((0, 16), (1, 2)))
    w_down = bell_draw(splits[12], (FF, D), FF ** -0.5, 0.109375, ((0, 2), (1, 16)))
    cotangent = bell_draw(splits[13], (TOKENS, D), 1.0, 6.0, ((0, 32),))
    return dict(tokens=tokens, lengths=lengths, w_in=w_in, w_out=w_out, short_conv=short_conv, cond_conv=cond_conv, cond_gain=cond_gain, base_spectrum=base_spectrum, gain1=gain1, gain2=gain2, w_gate=w_gate, w_up=w_up, w_down=w_down, cotangent=cotangent)


EPS = 1e-05

@jax.custom_vjp
def low(v):
    return lax.optimization_barrier(v.astype(jnp.bfloat16)).astype(jnp.float32)

@jax.custom_vjp
def low_back(v):
    return v

def low_keep(v):
    return (low(v), None)

def low_pass(kept, grad):
    return (grad,)

def back_keep(v):
    return (v, None)

def back_low(kept, grad):
    return (low(grad),)
low.defvjp(low_keep, low_pass)
low_back.defvjp(back_keep, back_low)

def layer_norm(values, gain):
    centre = values - lax.optimization_barrier(jnp.mean(values, axis=-1, keepdims=True))
    var = lax.optimization_barrier(jnp.mean(centre * centre, axis=-1, keepdims=True))
    return centre * lax.rsqrt(var + EPS) * gain

def matmul(left, right):
    return jnp.dot(left, right, precision=lax.Precision.HIGHEST, preferred_element_type=jnp.float32)

def causal_taps(seq, taps):
    one = jnp.pad(seq, ((0, 0), (1, 0), (0, 0)))[:, :-1]
    two = jnp.pad(seq, ((0, 0), (2, 0), (0, 0)))[:, :-2]
    return taps[0] * seq + taps[1] * one + taps[2] * two

def forward(tokens, w_in, w_out, short_conv, cond_conv, cond_gain, base_spectrum, gain1, gain2, w_gate, w_up, w_down, mask):
    groups = tokens.shape[0] // LENGTH
    width = tokens.shape[1]
    mask3 = mask.reshape(groups, LENGTH, 1)
    normed = low(layer_norm(tokens, gain1) * mask)
    streams = low_back(matmul(normed, w_in))
    conv_in = causal_taps(streams.reshape(groups, LENGTH, 3 * width), short_conv)
    gate_a = conv_in[:, :, :width]
    cond_b = conv_in[:, :, width:2 * width]
    values = conv_in[:, :, 2 * width:] * mask3
    cond_k = causal_taps(cond_b, cond_conv) * mask3
    spec_k = jnp.fft.rfft(cond_k, n=2 * LENGTH, axis=1)
    spec_v = jnp.fft.rfft(values, n=2 * LENGTH, axis=1)
    kr, ki = (jnp.real(spec_k), jnp.imag(spec_k))
    vr, vi = (jnp.real(spec_v), jnp.imag(spec_v))
    filt_r = base_spectrum[0] + cond_gain[0] * kr - cond_gain[1] * ki
    filt_i = base_spectrum[1] + cond_gain[0] * ki + cond_gain[1] * kr
    prod_r = vr * filt_r - vi * filt_i
    prod_i = vr * filt_i + vi * filt_r
    conv = jnp.fft.irfft(lax.complex(prod_r, prod_i), n=2 * LENGTH, axis=1)[:, :LENGTH]
    gated = low((gate_a * conv * mask3).reshape(groups * LENGTH, width))
    x_one = tokens + low_back(matmul(gated, w_out))
    normed_two = low(layer_norm(x_one, gain2) * mask)
    gate = low_back(matmul(normed_two, w_gate))
    upper = low_back(matmul(normed_two, w_up))
    act = low(jax.nn.gelu(gate, approximate=False) * upper)
    return x_one + low_back(matmul(act, w_down))

def reference(tokens, lengths, w_in, w_out, short_conv, cond_conv, cond_gain, base_spectrum, gain1, gain2, w_gate, w_up, w_down, cotangent):
    weights = tuple((w.astype(jnp.float32) for w in (w_in, w_out, short_conv, cond_conv, cond_gain, base_spectrum, gain1, gain2, w_gate, w_up, w_down)))
    group = math.gcd(SEQS, max(1, 4096 // LENGTH))
    blocks = SEQS // group
    positions = jnp.arange(LENGTH, dtype=jnp.int32)
    mask = (positions[None, :] < lengths[:, None]).astype(jnp.float32).reshape(blocks, group * LENGTH, 1)
    xs = tokens.astype(jnp.float32).reshape(blocks, group * LENGTH, D)
    cs = cotangent.astype(jnp.float32).reshape(blocks, group * LENGTH, D)

    def one_block(carry, item):
        x_blk, m_blk, c_blk = item

        def local(x_in, *ws):
            return forward(x_in, *ws, m_blk)
        out, pull = jax.vjp(local, x_blk, *weights)
        grads = pull(c_blk)
        carry = tuple((a + b for a, b in zip(carry, grads[1:])))
        return (carry, (out, grads[0]))
    init = tuple((jnp.zeros(w.shape, jnp.float32) for w in weights))
    totals, (outs, dxs) = lax.scan(one_block, init, (xs, mask, cs))
    mixed = outs.reshape(TOKENS, D).astype(jnp.bfloat16)
    grad_tokens = dxs.reshape(TOKENS, D)
    return (mixed, grad_tokens, totals[0], totals[1], totals[2], totals[3], totals[4], totals[5], totals[6], totals[7], totals[8], totals[9], totals[10])
```

```python
import functools
import math

import jax
import jax.numpy as jnp
import numpy as np
from jax import lax
from jax.experimental import pallas as pl
from jax.experimental.pallas import tpu as pltpu
from jax.sharding import PartitionSpec as P

EPS = 1e-05
AXES = ("dp", "mp")
F32 = jnp.float32
BF16 = jnp.bfloat16
NN = (((1,), (0,)), ((), ()))
NT = (((1,), (1,)), ((), ()))
TN = (((0,), (0,)), ((), ()))
RSQRT2 = np.float32(math.sqrt(0.5))
RSQRT2PI = np.float32(1.0 / math.sqrt(2.0 * math.pi))
CB = 256
RB = 256
VMEM = pl.BlockSpec(memory_space=pltpu.VMEM)
SMEM = pl.BlockSpec(memory_space=pltpu.SMEM)
ANY = pl.BlockSpec(memory_space=pl.ANY)


def dot(left, right, dims=NN):
    return lax.dot_general(left, right, dims, preferred_element_type=F32)


def sds(shape, dtype):
    return jax.ShapeDtypeStruct(shape, dtype)


def params(name=None):
    return pltpu.CompilerParams(vmem_limit_bytes=58 * 2**20)


def cost(flops, nbytes):
    return pl.CostEstimate(flops=int(flops), bytes_accessed=int(nbytes), transcendentals=0)


class Plan:
    def __init__(self, ndp, nmp):
        self.ndp, self.nmp, self.n = ndp, nmp, ndp * nmp
        self.core = nmp
        self.y = [0, nmp * 2] if ndp >= 4 else [0]
        self.z = [nmp * 4 * k for k in range(ndp // 4)]
        self.x = list(range(nmp))

    def send(self, array, mask):
        return lax.ppermute(array, AXES, [(i, i ^ mask) for i in range(self.n)])

    def gather(self, own, route):
        cur, order = own[None], [0]
        for group in route:
            parts = [cur] + [self.send(cur, m) for m in group[1:]]
            cur = jnp.concatenate(parts, axis=0) if len(parts) > 1 else cur
            order = [o ^ m for m in group for o in order]
        return cur, self.send(cur, self.core), order

    def gather_rows(self, own, route, mp_index):
        cur, order = own[None], [0]
        for group in route:
            parts = [cur] + [self.send(cur, m) for m in group[1:]]
            if group is self.x:
                step = 1
                while step < self.nmp:
                    odd = (mp_index & step) != 0
                    parts = [jnp.where(odd, parts[k ^ step], parts[k]) for k in range(self.nmp)]
                    step *= 2
                cur = jnp.concatenate(parts, axis=1)
            else:
                cur = jnp.concatenate(parts, axis=0)
                order = [o ^ m for m in group for o in order]
        return cur, self.send(cur, self.core), [o // self.nmp for o in order]

    def route_order(self, route, with_x):
        order = [0]
        for group in route:
            if group is self.x and not with_x:
                continue
            order = [o ^ m for o in order for m in group]
        return order if with_x else [o // self.nmp for o in order]

    def scatter(self, keep, far, route):
        total = keep.astype(F32) + self.send(far, self.core).astype(F32)
        for group in route:
            total = total.reshape((len(group), -1) + total.shape[1:])
            got = [self.send(total[k].astype(BF16), m) for k, m in enumerate(group) if m]
            total = sum([g.astype(F32) for g in got], total[0])
        return total.reshape(total.shape[1:])

    def scatter_rows(self, keep, far, route, mp_index):
        total = keep.astype(F32) + self.send(far, self.core).astype(F32)
        for group in route:
            if group is self.x:
                rows = total.shape[1] // self.nmp
                part = lambda m: lax.dynamic_slice_in_dim(total, (mp_index ^ m) * rows, rows, axis=1)
                got = [self.send(part(m).astype(BF16), m) for m in group[1:]]
                total = sum([g.astype(F32) for g in got], part(0))
            else:
                total = total.reshape((len(group), -1) + total.shape[1:])
                got = [self.send(total[k].astype(BF16), m) for k, m in enumerate(group) if m]
                total = sum([g.astype(F32) for g in got], total[0])
        return total.reshape(total.shape[1:])


def shift_down(value, count, row):
    return jnp.where(row >= count, pltpu.roll(value, count, 0), 0.0)


def shift_up(value, count, row):
    length = value.shape[0]
    return jnp.where(row < length - count, pltpu.roll(value, length - count, 0), 0.0)


def taps(value, w, row):
    return w[0:1] * value + w[1:2] * shift_down(value, 1, row) + w[2:3] * shift_down(value, 2, row)


def taps_back(grad, w, row):
    one, two = shift_up(grad, 1, row), shift_up(grad, 2, row)
    return w[0:1] * grad + w[1:2] * one + w[2:3] * two, one, two


def tap_sums(grads, value):
    return jnp.concatenate([jnp.sum(g * value, axis=0, keepdims=True) for g in grads], axis=0)


def normalise(value):
    centre = value - jnp.mean(value, axis=-1, keepdims=True)
    scale = lax.rsqrt(jnp.mean(centre * centre, axis=-1, keepdims=True) + EPS)
    return centre * scale, scale


def normalise_back(grad, unit, scale, gain):
    dx = grad * gain
    first = jnp.mean(dx, axis=-1, keepdims=True)
    second = jnp.mean(dx * unit, axis=-1, keepdims=True)
    return scale * (dx - first - unit * second)


def row_mask(lens, start, rows, length):
    seq = start // length
    base = start - seq * length
    return ((lax.broadcasted_iota(jnp.int32, (rows, 1), 0) + base) < lens[seq]).astype(F32)


def cmul(pr, pi, qr, qi, slot0):
    cross = pi * qi
    return pr * qr - jnp.where(slot0, 0.0, cross), jnp.where(slot0, cross, pr * qi + pi * qr)


def cmul_conj(pr, pi, qr, qi, slot0):
    cross = pi * qi
    return pr * qr + jnp.where(slot0, 0.0, cross), jnp.where(slot0, cross, pi * qr - pr * qi)


def load_rows(dst, near, far, order, dp_ref, rows, sems):
    if order is None:
        return [pltpu.make_async_copy(near, dst, sems.at[0])]
    out = []
    for s, rel in enumerate(order):
        for k, src in enumerate((near, far)):
            at = pl.multiple_of((dp_ref[0] ^ (rel ^ k)) * rows, rows)
            out.append(pltpu.make_async_copy(src.at[s], dst.at[pl.ds(at, rows)], sems.at[2 * s + k]))
    return out


def store_rows(src, near, far, order, dp_ref, rows, cols, sems):
    out = []
    for s, rel in enumerate(order):
        for k, dst in enumerate((near, far)):
            at = pl.multiple_of((dp_ref[0] ^ (rel ^ k)) * rows, rows)
            out.append(pltpu.make_async_copy(src.at[pl.ds(at, rows), cols], dst.at[s], sems.at[2 * s + k]))
    return out


def mixer_in_kernel(order, rows, length, dp, lens, x, gain, short, cond, tab, near, far, n1, z, kk, vv, w_full, w, sems, wsem):
    copies = load_rows(w, near, far, order, dp, rows, sems)
    for c in copies:
        c.start()
    tokens, width = x.shape
    keep = pltpu.make_async_copy(w.at[:, pl.ds(0, 3 * width)], w_full, wsem)

    @pl.loop(0, tokens // RB)
    def _(m):
        start = pl.multiple_of(m * RB, RB)
        unit, _ = normalise(x[pl.ds(start, RB), :].astype(F32))
        n1[pl.ds(start, RB), :] = (unit * gain[...] * row_mask(lens, start, RB, length)).astype(BF16)

    for c in copies:
        c.wait()
    keep.start()
    row = lax.broadcasted_iota(jnp.int32, (length, 1), 0)
    blocks = width // CB

    @pl.loop(0, blocks * (tokens // length))
    def _(step):
        seq, cb = step // blocks, lax.rem(step, blocks)
        rs = pl.ds(pl.multiple_of(seq * length, length), length)
        mask = (row < lens[seq]).astype(F32)
        zs = []
        for stream in (1, 2, 0):
            cs = pl.ds(pl.multiple_of(stream * width + cb * CB, CB), CB)
            val = dot(n1[rs, :], w[:, cs])
            z[rs, cs] = val.astype(BF16)
            if stream:
                zs.append(taps(val, short[:, cs], row))
        cs = pl.ds(pl.multiple_of(cb * CB, CB), CB)
        k = taps(zs[0], cond[:, cs], row) * mask
        kk[seq, :, cs] = dot(tab[...], k.astype(BF16)).astype(BF16)
        vv[seq, :, cs] = dot(tab[...], (zs[1] * mask).astype(BF16)).astype(BF16)

    keep.wait()


def filtered(half, spec, kr, ki, slot0):
    br, bi, gr, gi = (spec[n * half : (n + 1) * half, :] for n in range(4))
    tr, ti = cmul(gr, gi, kr, ki, slot0)
    return br + tr, bi + ti, gr, gi


def mixer_out_kernel(order, rows, length, dp, lens, x, gain, short, tabt, kk, vv, z, near, far, o, conv, x1, n2, spec_t, w_out, g2, sems):
    copies = load_rows(g2, near, far, order, dp, rows, sems)
    for c in copies:
        c.start()
    tokens, width = x.shape
    half = length
    for c in copies:
        c.wait()
    row = lax.broadcasted_iota(jnp.int32, (length, 1), 0)
    slot0 = row == 0
    scale = jnp.where(slot0, 1.0, 2.0) * np.float32(0.5 / length)
    w_out[...] = g2[:, :width]

    @pl.loop(0, width // CB)
    def _(cb):
        cs = pl.ds(pl.multiple_of(cb * CB, CB), CB)
        spec = jnp.transpose(g2[cs, width:].astype(F32), (1, 0))
        spec_t[:, cs] = spec.astype(BF16)
        for seq in range(tokens // length):
            rs = slice(seq * length, (seq + 1) * length)
            kr, ki = kk[seq, :half, cs].astype(F32), kk[seq, half:, cs].astype(F32)
            vr, vi = vv[seq, :half, cs].astype(F32), vv[seq, half:, cs].astype(F32)
            hr, hi, _, _ = filtered(half, spec, kr, ki, slot0)
            yr, yi = cmul(vr, vi, hr, hi, slot0)
            y = jnp.concatenate([(yr * scale).astype(BF16), (yi * scale).astype(BF16)], axis=0)
            out = dot(tabt[...], y)
            conv[rs, cs] = out.astype(BF16)
            a = taps(z[rs, cs].astype(F32), short[:, cs], row)
            o[rs, cs] = (a * out * (row < lens[seq]).astype(F32)).astype(BF16)

    @pl.loop(0, tokens // RB)
    def _(m):
        start = pl.multiple_of(m * RB, RB)
        rs = pl.ds(start, RB)
        val = x[rs, :].astype(F32) + dot(o[rs, :], w_out[...])
        x1[rs, :] = val
        unit, _ = normalise(val)
        n2[rs, :] = (unit * gain[...] * row_mask(lens, start, RB, length)).astype(BF16)


def ffn_kernel(orders, rows, first, dp, n2, c, *refs):
    parts = len(orders)
    refs = list(refs)
    acc_in, dn_in = (None, None) if first else (refs.pop(0), refs.pop(0))
    gathered = [(refs.pop(0), refs.pop(0)) for _ in range(parts)]
    acc, dn = refs.pop(0), refs.pop(0)
    outs = [(refs.pop(0), refs.pop(0)) for _ in range(parts)]
    w, g, act, dg, du, sem_in, sem_out = refs
    tokens = n2.shape[0]
    hidden = w.shape[3]
    loads, stores = [], []
    for p, (gather_order, scatter_order) in enumerate(orders):
        cols = gathered[p][0].shape[3]
        nmp = hidden // cols
        ins, out = [], []
        for s, rel in enumerate(gather_order):
            for k, src in enumerate(gathered[p]):
                at = pl.multiple_of((dp[0] ^ ((rel // nmp) ^ k)) * rows, rows)
                ins.append(pltpu.make_async_copy(src.at[s], w.at[p, :, pl.ds(at, rows), pl.ds((rel % nmp) * cols, cols)], sem_in.at[p, 2 * s + k]))
        for s, rel in enumerate(scatter_order):
            for k, dst in enumerate(outs[p]):
                at = pl.multiple_of((dp[0] ^ ((rel // nmp) ^ k)) * rows, rows)
                out.append(pltpu.make_async_copy(g.at[p, :, pl.ds(at, rows), pl.ds((rel % nmp) * cols, cols)], dst.at[s], sem_out.at[p, 2 * s + k]))
        loads.append(ins)
        stores.append(out)
    for ins in loads:
        for copy in ins:
            copy.start()
    for p in range(parts):
        for copy in loads[p]:
            copy.wait()

        @pl.loop(0, hidden // 256)
        def _(h):
            hs = pl.ds(pl.multiple_of(h * 256, 256), 256)

            @pl.loop(0, tokens // 512)
            def _(m):
                ms = pl.ds(pl.multiple_of(m * 512, 512), 512)
                gate = dot(n2[ms, :], w[p, 0, :, hs])
                up = dot(n2[ms, :], w[p, 1, :, hs])
                dact = dot(c[ms, :], w[p, 2, :, hs])
                cdf = 0.5 + 0.5 * lax.erf(gate * RSQRT2)
                soft = gate * cdf
                slope = cdf + gate * (jnp.exp(-0.5 * gate * gate) * RSQRT2PI)
                act[ms, hs] = (soft * up).astype(BF16)
                dg[ms, hs] = (dact * up * slope).astype(BF16)
                du[ms, hs] = (dact * soft).astype(BF16)

        @pl.loop(0, hidden // 256)
        def _(h):
            hs = pl.ds(pl.multiple_of(h * 256, 256), 256)
            g[p, 0, :, hs] = dot(n2[...], dg[:, hs], TN).astype(BF16)
            g[p, 1, :, hs] = dot(n2[...], du[:, hs], TN).astype(BF16)
            g[p, 2, :, hs] = dot(c[...], act[:, hs], TN).astype(BF16)

        for copy in stores[p]:
            copy.start()

        @pl.loop(0, tokens // RB)
        def _(m):
            ms = pl.ds(pl.multiple_of(m * RB, RB), RB)
            out = dot(act[ms, :], w[p, 2], NT)
            back = dot(dg[ms, :], w[p, 0], NT) + dot(du[ms, :], w[p, 1], NT)
            if p == 0 and first:
                acc[ms, :] = out
                dn[ms, :] = back
            elif p == 0:
                acc[ms, :] = acc_in[ms, :] + out
                dn[ms, :] = dn_in[ms, :] + back
            else:
                acc[ms, :] += out
                dn[ms, :] += back

    for out in stores:
        for copy in out:
            copy.wait()


def spectrum_back_kernel(order, rows, length, dp, lens, x1, acc, dn, c, gain, o, w_out, spec_t, kk, vv, z, conv, short, tab,
                         mixed, dx1, d_gain, dk, dv, da, near, far, dm1, g2, sems):
    tokens, width = x1.shape
    half = length
    d_gain[...] = jnp.zeros_like(d_gain)

    @pl.loop(0, tokens // RB)
    def _(m):
        start = pl.multiple_of(m * RB, RB)
        rs = pl.ds(start, RB)
        mixed[rs, :] = (x1[rs, :] + acc[rs, :]).astype(BF16)
        unit, scale = normalise(x1[rs, :])
        grad = dn[rs, :] * row_mask(lens, start, RB, length)
        d_gain[...] += jnp.sum(grad * unit, axis=0, keepdims=True)
        val = c[rs, :].astype(F32) + normalise_back(grad, unit, scale, gain[...])
        dx1[rs, :] = val
        dm1[rs, :] = val.astype(BF16)

    @pl.loop(0, width // CB)
    def _(cb):
        cs = pl.ds(pl.multiple_of(cb * CB, CB), CB)
        g2[:, cs] = dot(o[...], dm1[:, cs], TN).astype(BF16)

    row = lax.broadcasted_iota(jnp.int32, (length, 1), 0)
    slot0 = row == 0
    scale = jnp.where(slot0, 1.0, 2.0) * np.float32(0.5 / length)

    @pl.loop(0, width // CB)
    def _(cb):
        cs = pl.ds(pl.multiple_of(cb * CB, CB), CB)
        spec = spec_t[:, cs].astype(F32)
        sums = [0.0] * 4
        for seq in range(tokens // length):
            rs = slice(seq * length, (seq + 1) * length)
            d_o = dot(dm1[rs, :], w_out[cs, :], NT) * (row < lens[seq]).astype(F32)
            da[rs, cs] = (d_o * conv[rs, cs].astype(F32)).astype(BF16)
            a = taps(z[rs, cs].astype(F32), short[:, cs], row)
            dy = dot(tab[...], (d_o * a).astype(BF16))
            dyr, dyi = dy[:half] * scale, dy[half:] * scale
            kr, ki = kk[seq, :half, cs].astype(F32), kk[seq, half:, cs].astype(F32)
            vr, vi = vv[seq, :half, cs].astype(F32), vv[seq, half:, cs].astype(F32)
            hr, hi, gr, gi = filtered(half, spec, kr, ki, slot0)
            dvr, dvi = cmul_conj(dyr, dyi, hr, hi, slot0)
            dv[seq, :half, cs], dv[seq, half:, cs] = dvr.astype(BF16), dvi.astype(BF16)
            dhr, dhi = cmul_conj(dyr, dyi, vr, vi, slot0)
            dkr, dki = cmul_conj(dhr, dhi, gr, gi, slot0)
            dk[seq, :half, cs], dk[seq, half:, cs] = dkr.astype(BF16), dki.astype(BF16)
            ggr, ggi = cmul_conj(dhr, dhi, kr, ki, slot0)
            sums = [s + t for s, t in zip(sums, (dhr, dhi, ggr, ggi))]
        for n, val in enumerate(sums):
            g2[cs, width + n * half : width + (n + 1) * half] = jnp.transpose(val, (1, 0)).astype(BF16)

    copies = store_rows(g2, near, far, order, dp, rows, slice(None), sems)
    for copy in copies:
        copy.start()
    for copy in copies:
        copy.wait()


def mixer_back_kernel(orders, rows, length, dp, lens, n1, z, dk, dv, da, short, cond, tabt, *refs):
    parts = len(orders)
    dz, d_short, d_cond = refs[:3]
    outs = [refs[3 + 2 * p : 5 + 2 * p] for p in range(parts)]
    g, sems = refs[3 + 2 * parts :]
    tokens, width = n1.shape
    row = lax.broadcasted_iota(jnp.int32, (length, 1), 0)
    d_short[...] = jnp.zeros_like(d_short)
    d_cond[...] = jnp.zeros_like(d_cond)

    @pl.loop(0, width // CB)
    def _(cb):
        for seq in range(tokens // length):
            rs = slice(seq * length, (seq + 1) * length)
            cols = [pl.ds(pl.multiple_of(n * width + cb * CB, CB), CB) for n in range(3)]
            cs = cols[0]
            mask = (row < lens[seq]).astype(F32)
            dvm = dot(tabt[...], dv[seq, :, cs]) * mask
            dkm = dot(tabt[...], dk[seq, :, cs]) * mask
            zb = z[rs, cols[1]].astype(F32)
            b = taps(zb, short[:, cols[1]], row)
            db, one, two = taps_back(dkm, cond[:, cs], row)
            d_cond[:, cs] += tap_sums((dkm, one, two), b)
            for n, grad in enumerate((da[rs, cs].astype(F32), db, dvm)):
                val, one, two = taps_back(grad, short[:, cols[n]], row)
                zn = zb if n == 1 else z[rs, cols[n]].astype(F32)
                d_short[:, cols[n]] += tap_sums((grad, one, two), zn)
                dz[rs, cols[n]] = val.astype(BF16)

    @pl.loop(0, 3 * width // CB)
    def _(cb):
        cs = pl.ds(pl.multiple_of(cb * CB, CB), CB)
        g[:, cs] = dot(n1[...], dz[:, cs], TN).astype(BF16)

    copies, at = [], 0
    for p in range(parts):
        cols = outs[p][0].shape[2]
        copies += store_rows(g, *outs[p], orders[p], dp, rows, pl.ds(at, cols), sems.at[p])
        at += cols
    for copy in copies:
        copy.start()
    for copy in copies:
        copy.wait()


def token_back_kernel(length, lens, x, dz, w, dx1, gain, grad, d_gain):
    tokens, width = x.shape
    d_gain[...] = jnp.zeros_like(d_gain)

    @pl.loop(0, tokens // RB)
    def _(m):
        start = pl.multiple_of(m * RB, RB)
        rs = pl.ds(start, RB)
        d_n1 = dot(dz[rs, :], w[...], NT) * row_mask(lens, start, RB, length)
        unit, scale = normalise(x[rs, :].astype(F32))
        d_gain[...] += jnp.sum(d_n1 * unit, axis=0, keepdims=True)
        grad[rs, :] = dx1[rs, :] + normalise_back(d_n1, unit, scale, gain[...])


def dft_table(length):
    phase = np.outer(np.arange(length), np.arange(length)) % (2 * length)
    angle = phase * (math.pi / length)
    real, imag = np.cos(angle), -np.sin(angle)
    imag[0] = np.cos(math.pi * np.arange(length))
    return np.concatenate([real, imag], axis=0).astype(np.float32).astype(jnp.bfloat16)


def pack_spectrum(spec, half):
    return jnp.concatenate([spec[0, :half], spec[0, half:], spec[1, 1:half]], axis=0).T


def unpack_spectrum(flat, half):
    real, imag = flat[:, :half].T, flat[:, half:].T
    zero = jnp.zeros_like(real[:1])
    return jnp.stack([jnp.concatenate([real, imag[:1]], axis=0), jnp.concatenate([zero, imag[1:], zero], axis=0)])


def shards(ndp, nmp, tokens, lengths, w_in, w_out, short_conv, cond_conv, cond_gain, base_spectrum, gain1, gain2, w_gate, w_up, w_down, cotangent):
    plan = Plan(ndp, nmp)
    rows_all, width = tokens.shape
    seqs = lengths.shape[0]
    length = rows_all // seqs
    half = length
    dp_index, mp_index = lax.axis_index("dp"), lax.axis_index("mp")
    dp = dp_index.reshape(1).astype(jnp.int32)
    routes = ((plan.z, plan.y, plan.x), (plan.z, plan.x, plan.y))
    back_routes = ((plan.y, plan.x, plan.z), (plan.x, plan.y, plan.z))

    small = jnp.concatenate([short_conv.reshape(-1), cond_conv.reshape(-1), gain1, gain2])
    chan = w_in.shape[0]
    slots = small.shape[0] // chan
    small = jnp.pad(small.reshape(chan, slots), ((0, 0), (0, 128 - slots)))
    own1 = jnp.concatenate([w_in, small], axis=1)
    own2 = jnp.concatenate([w_out, pack_spectrum(base_spectrum, half), pack_spectrum(cond_gain, half)], axis=1)
    ffn = jnp.stack([w_gate, w_up, w_down.T])
    rows = width // ndp
    group = ffn.shape[2]
    split = 384 if group % 1536 == 0 else 128
    pieces = [ffn[:, :, k : k + split] for k in range(0, group, split)]

    near1, far1, order1 = plan.gather_rows(own1, routes[0], mp_index)
    near2, far2, order2 = plan.gather_rows(own2, routes[1], mp_index)
    gathered = [plan.gather(piece, routes[k % 2]) for k, piece in enumerate(pieces)]

    full = jnp.concatenate([near1[:, :, 3 * width :], far1[:, :, 3 * width :]], axis=0).astype(F32)
    rel = jnp.array(order1 + [r ^ 1 for r in order1], jnp.int32)
    hot = (rel[None, :] == (jnp.arange(ndp, dtype=jnp.int32) ^ dp_index)[:, None]).astype(F32)
    full = jnp.dot(hot, full[:, :, :slots].reshape(ndp, -1), precision=lax.Precision.HIGHEST)
    full = full.reshape(ndp * nmp, chan * slots)
    cuts = np.cumsum([short_conv.size, cond_conv.size, chan])
    short = full[:, : cuts[0]].reshape(-1, 3, 3 * chan).transpose(1, 0, 2).reshape(3, 3 * width)
    cond = full[:, cuts[0] : cuts[1]].reshape(-1, 3, chan).transpose(1, 0, 2).reshape(3, width)
    gain_one = full[:, cuts[1] : cuts[2]].reshape(1, width)
    gain_two = full[:, cuts[2] :].reshape(1, width)

    if rows % 16:

        def whole(near, far, order):
            both = jnp.concatenate([near, far], axis=0)
            index = jnp.array(order + [r ^ 1 for r in order], jnp.int32)
            place = jnp.argsort(index ^ dp_index)
            return jnp.take(both, place, axis=0).reshape(width, -1)

        near1 = whole(near1, far1, order1)
        near2 = whole(near2, far2, order2)
        order1 = order2 = None

    tab = jnp.asarray(dft_table(length))
    tabt = jnp.asarray(dft_table(length).T)
    sems = pltpu.SemaphoreType.DMA((ndp,))
    spectra = sds((seqs, 2 * half, width), BF16)

    n1, z, kk, vv, w_full = pl.pallas_call(
        functools.partial(mixer_in_kernel, order1, rows, length),
        out_shape=[sds((rows_all, width), BF16), sds((rows_all, 3 * width), BF16), spectra, spectra, sds((width, 3 * width), BF16)],
        in_specs=[SMEM, SMEM, VMEM, VMEM, VMEM, VMEM, VMEM, ANY, ANY],
        out_specs=[VMEM, VMEM, VMEM, VMEM, ANY],
        scratch_shapes=[pltpu.VMEM((width, 3 * width + 128), BF16), sems, pltpu.SemaphoreType.DMA],
        compiler_params=params(),
        cost_estimate=cost(2 * rows_all * width * (3 * width + 4 * half), 30e6),
        name="mixer_in",
    )(dp, lengths, tokens, gain_one, short, cond, tab, near1, far1)

    cols2 = width + 4 * half
    o, conv, x1, n2, spec_t, w_out_full = pl.pallas_call(
        functools.partial(mixer_out_kernel, order2, rows, length),
        out_shape=[sds((rows_all, width), BF16), sds((rows_all, width), BF16), sds((rows_all, width), F32), sds((rows_all, width), BF16),
                   sds((4 * half, width), BF16), sds((width, width), BF16)],
        in_specs=[SMEM, SMEM, VMEM, VMEM, VMEM, VMEM, VMEM, VMEM, VMEM, ANY, ANY],
        out_specs=[VMEM] * 6,
        scratch_shapes=[pltpu.VMEM((width, cols2), BF16), sems],
        compiler_params=params(),
        cost_estimate=cost(2 * rows_all * width * (width + 2 * half), 30e6),
        name="mixer_out",
    )(dp, lengths, tokens, gain_two, short, tabt, kk, vv, z, near2, far2)

    calls = [[k, k + 1] if k + 1 < len(pieces) else [k] for k in range(0, len(pieces), 2)]
    state = []
    ffn_grads = [None] * len(pieces)
    hidden = split * nmp
    for call in calls:
        orders = [(gathered[k][2], plan.route_order(back_routes[k % 2], True)) for k in call]
        blocks = [a for k in call for a in gathered[k][:2]]
        count = len(call)
        got = pl.pallas_call(
            functools.partial(ffn_kernel, orders, rows, not state),
            out_shape=[sds((rows_all, width), F32)] * 2 + [sds(a.shape, BF16) for a in blocks],
            in_specs=[SMEM, VMEM, VMEM] + [VMEM] * len(state) + [ANY] * (2 * count),
            out_specs=[VMEM, VMEM] + [ANY] * (2 * count),
            scratch_shapes=[pltpu.VMEM((count, 3, width, hidden), BF16)] * 2 + [pltpu.VMEM((rows_all, hidden), BF16)] * 3
            + [pltpu.SemaphoreType.DMA((count, ndp * nmp))] * 2,
            compiler_params=params(),
            cost_estimate=cost(18 * rows_all * width * hidden * count, 30e6),
            name="ffn",
        )(dp, n2, cotangent, *state, *blocks)
        state = got[:2]
        for j, k in enumerate(call):
            ffn_grads[k] = got[2 + 2 * j : 4 + 2 * j]
    acc, dn = state
    sums = [plan.scatter(near, far, back_routes[k % 2]) for k, (near, far) in enumerate(ffn_grads)]
    grad_ffn = jnp.concatenate(sums, axis=2)

    g2_order = plan.route_order(back_routes[1], False)
    cube = sds((ndp // 2, rows, cols2), BF16)
    mixed, dx1, d_gain2, dk, dv, da, near, far = pl.pallas_call(
        functools.partial(spectrum_back_kernel, g2_order, rows, length),
        out_shape=[sds((rows_all, width), BF16), sds((rows_all, width), F32), sds((1, width), F32), spectra, spectra,
                   sds((rows_all, width), BF16), cube, cube],
        in_specs=[SMEM, SMEM] + [VMEM] * 14,
        out_specs=[VMEM] * 6 + [ANY] * 2,
        scratch_shapes=[pltpu.VMEM((rows_all, width), BF16), pltpu.VMEM((width, cols2), BF16), sems],
        compiler_params=params(),
        cost_estimate=cost(2 * rows_all * width * (2 * width + 2 * half), 40e6),
        name="spectrum_back",
    )(dp, lengths, x1, acc, dn, cotangent, gain_two, o, w_out_full, spec_t, kk, vv, z, conv, short, tab)
    grad2 = plan.scatter_rows(near, far, back_routes[1], mp_index)

    cols = (3 * width) // 2
    orders = [plan.route_order(route, False) for route in back_routes]
    cube = sds((ndp // 2, rows, cols), BF16)
    dz, d_short, d_cond, *blocks = pl.pallas_call(
        functools.partial(mixer_back_kernel, orders, rows, length),
        out_shape=[sds((rows_all, 3 * width), BF16), sds((3, 3 * width), F32), sds((3, width), F32)] + [cube] * 4,
        in_specs=[SMEM, SMEM] + [VMEM] * 8,
        out_specs=[VMEM] * 3 + [ANY] * 4,
        scratch_shapes=[pltpu.VMEM((width, 3 * width), BF16), pltpu.SemaphoreType.DMA((2, ndp))],
        compiler_params=params(),
        cost_estimate=cost(2 * rows_all * width * (3 * width + 4 * half), 30e6),
        name="mixer_back",
    )(dp, lengths, n1, z, dk, dv, da, short, cond, tabt)
    grad_in = jnp.concatenate(
        [plan.scatter_rows(blocks[2 * p], blocks[2 * p + 1], back_routes[p], mp_index) for p in range(2)], axis=1
    )

    grad_tokens, d_gain1 = pl.pallas_call(
        functools.partial(token_back_kernel, length),
        out_shape=[sds((rows_all, width), F32), sds((1, width), F32)],
        in_specs=[SMEM] + [VMEM] * 5,
        out_specs=[VMEM] * 2,
        compiler_params=params(),
        cost_estimate=cost(2 * rows_all * width * 3 * width, 20e6),
        name="token_back",
    )(lengths, tokens, dz, w_full, dx1, gain_one)

    flat = jnp.concatenate(
        [
            d_short.reshape(3, ndp * nmp, 3 * chan).transpose(1, 0, 2).reshape(ndp * nmp, -1),
            d_cond.reshape(3, ndp * nmp, chan).transpose(1, 0, 2).reshape(ndp * nmp, -1),
            d_gain1.reshape(-1, chan),
            d_gain2.reshape(-1, chan),
        ],
        axis=1,
    )
    me = dp_index * nmp + mp_index
    order = plan.route_order(back_routes[0], True)
    order = jnp.array(order + [r ^ plan.core for r in order], jnp.int32)
    hot = ((order ^ me)[:, None] == jnp.arange(ndp * nmp, dtype=jnp.int32)[None, :]).astype(F32)
    flat = jnp.dot(hot, flat, precision=lax.Precision.HIGHEST)
    count = ndp * nmp // 2
    total = flat[:count] + plan.send(flat[count:], plan.core)
    for grp in back_routes[0]:
        total = total.reshape((len(grp), -1) + total.shape[1:])
        total = sum([plan.send(total[k], m) for k, m in enumerate(grp) if m], total[0])
    total = total.reshape(-1)
    cuts = np.cumsum([short_conv.size, cond_conv.size, chan])

    return (
        mixed,
        grad_tokens,
        grad_in,
        grad2[:, :width],
        total[: cuts[0]].reshape(short_conv.shape),
        total[cuts[0] : cuts[1]].reshape(cond_conv.shape),
        unpack_spectrum(grad2[:, width + 2 * half :], half),
        unpack_spectrum(grad2[:, width : width + 2 * half], half),
        total[cuts[1] : cuts[2]],
        total[cuts[2] :],
        grad_ffn[0],
        grad_ffn[1],
        grad_ffn[2].T,
    )


def solution(mesh):
    rows = P(AXES, None)
    cols = P(None, AXES)
    deep = P(None, None, AXES)
    flat = P(AXES)
    in_specs = (rows, flat, rows, rows, cols, cols, deep, deep, flat, flat, P("dp", "mp"), P("dp", "mp"), P("mp", "dp"), rows)
    out_specs = (rows, rows, rows, rows, cols, cols, deep, deep, flat, flat, P("dp", "mp"), P("dp", "mp"), P("mp", "dp"))
    body = functools.partial(shards, mesh.shape["dp"], mesh.shape["mp"])
    return jax.shard_map(body, mesh=mesh, in_specs=in_specs, out_specs=out_specs, check_vma=False)
```
